512 devices in a mesh: vox: 32 (over x_lo, z, core), sta: 16 (over x_hi, y).
Axes of the slice: x: 4 (x_hi: 2, x_lo: 2; x = x_hi * 2 + x_lo), y: 8, z: 8, core: 2. Of those that a mesh axis runs over, the one named last changes fastest.
Arguments:
- green_tensor: bfloat16 [16, 6, 256, 4096], P('sta', None, None, 'vox'), may hold values from -0.078125 to 0.078125
- strain: bfloat16 [32, 6, 256, 4096], P('sta', None, None, 'vox'), may hold values from -6 to 6
- pair_events: int32 [16, 32], P('sta'), may hold values from -1 to 31, as said below
- pair_counts: int32 [16], P('sta'), may hold values from 22 to 32, as said below
- residuals: float32 [16, 32, 256], P('sta'), may hold values from -0.375 to 0.375
Outputs:
- kernel: float32 [4096], P(('vox', 'sta'))
The draws below stay inside these ranges and needn't reach their ends.
Inputs may be any that keep to these rules, and one draw needn't show every extreme that they name: `pair_events`: within a station the live entries are distinct earthquakes; slots at or beyond the station's count hold -1. `pair_counts`: some station has exactly 32 live slots in every draw.
All inputs are finite; a program needn't handle non-finite values.
Results may differ from the reference program's by a relative error of at most 0.0029.
Values may be sent and summed in bfloat16 or wider, within the bound.
No kernel may reach another device: no remote copies, remote signals or barrier semaphores. Data moves between devices by JAX's collectives and lax.ppermute only.
A program may use at most 64 MiB of HBM per device.

```python
import jax
import jax.numpy as jnp
from jax import lax

COMP = 6
NT = 256
STATIONS = 16
EVENTS = 32
MAXP = 32
VOX = 4096


def pair_lists(key):
    first = jax.random.fold_in(key, 11)
    second = jax.random.fold_in(key, 12)
    third = jax.random.fold_in(key, 13)
    orders = jax.vmap(lambda k: jax.random.permutation(k, EVENTS))(jax.random.split(first, STATIONS))[:, :MAXP]
    drawn = jax.random.randint(second, (STATIONS,), 0, MAXP // 3 + 1)
    counts = MAXP - drawn
    busiest = jax.random.randint(third, (), 0, STATIONS)
    counts = jnp.where(jnp.arange(STATIONS) == busiest, MAXP, counts).astype(jnp.int32)
    places = jnp.arange(MAXP)[None, :]
    events = jnp.where(places < counts[:, None], orders, -1).astype(jnp.int32)
    return (events, counts)


def draw_pair_events(key, part):
    return pair_lists(key)[0]


def draw_pair_counts(key, part):
    return pair_lists(key)[1]


def shard_levels(own_key, shape, shards, smallest, top_value):
    factor_of = 1.0
    for dim, shards_of in shards:
        steps = jax.random.uniform(jax.random.fold_in(jax.random.fold_in(own_key, 6), dim), (shards_of,), jnp.float32, smallest / len(shards), top_value / len(shards))
        factor_of = factor_of * jnp.repeat(jnp.exp(steps), shape[dim] // shards_of).reshape((-1,) + (1,) * (len(shape) - 1 - dim))
    return factor_of


def noise(rng, shape, scale, bound, cuts=(), kind=jnp.bfloat16):
    array = scale * jax.random.normal(rng, shape, jnp.float32)
    if cuts:
        array = array * shard_levels(rng, shape, cuts, -0.22, 0.18)
    return jnp.clip(array, -bound, bound).astype(kind)


def setup_inputs(seed: int = 0) -> dict:
    arg_keys = jax.random.split(jax.random.key(seed), 6)
    return {
        "green_tensor": noise(arg_keys[0], (STATIONS, COMP, NT, VOX), (4 * COMP * NT) ** -0.5, 0.078125, ((0, 16), (3, 32))),
        "strain": noise(arg_keys[1], (EVENTS, COMP, NT, VOX), 1.0, 6.0, ((0, 16), (3, 32))),
        "pair_events": draw_pair_events(jax.random.fold_in(arg_keys[5], 71), 0),
        "pair_counts": draw_pair_counts(jax.random.fold_in(arg_keys[5], 71), 0),
        "residuals": noise(arg_keys[4], (STATIONS, MAXP, NT), NT ** -0.5, 0.375, ((0, 16),), jnp.float32),
    }


def toeplitz(wave):
    steps = jnp.arange(NT, dtype=jnp.int32)
    offset = steps[:, None] - steps[None, :]
    values = jnp.take(wave, jnp.clip(offset, 0, NT - 1), axis=-1)
    return jnp.where(offset >= 0, values, jnp.zeros_like(values))


def reference(green_tensor, strain, pair_events, pair_counts, residuals):
    def station(total, index):
        green = green_tensor[index].astype(jnp.float32)

        def slot(acc, place):
            event = pair_events[index, place]
            live = place < pair_counts[index]
            field = lax.dynamic_index_in_dim(strain, jnp.maximum(event, 0).astype(jnp.int32), 0, keepdims=False)
            matrix = toeplitz(residuals[index, place]).astype(jnp.bfloat16)
            conv = jnp.einsum("tu,cuv->ctv", matrix.astype(jnp.float32), field.astype(jnp.float32))
            term = jnp.sum(green * conv, axis=(0, 1))
            return acc + jnp.where(live, term, jnp.zeros_like(term)), None

        acc, _ = lax.scan(slot, total, jnp.arange(MAXP, dtype=jnp.int32))
        return acc, None

    start = jnp.zeros((VOX,), jnp.float32)
    kernel, _ = lax.scan(station, start, jnp.arange(STATIONS, dtype=jnp.int32))
    return kernel
```

```python
import jax
import jax.numpy as jnp
from jax import lax
from jax.experimental import pallas as pl
from jax.experimental.pallas import tpu as pltpu
from jax.sharding import PartitionSpec as P

COMP = 6
NT = 256
STA = 16
MAXP = 32
EVENTS = 32
OWN = 8
LAG = 32
BLOCKS = NT // LAG
S_COLS = COMP * 2 * NT
G_AT = S_COLS
R_AT = G_AT + COMP * NT
COLS = R_AT + (EVENTS // 8) * NT
F32 = jnp.float32
BF16 = jnp.bfloat16


def pack_kernel(counts_ref, green_ref, strain_ref, events_ref, resid_ref, out_ref):
    voxels = green_ref.shape[-1]
    for c in range(COMP):
        for half in range(2):
            rows = []
            for j in range(half * BLOCKS // 2, (half + 1) * BLOCKS // 2):
                for e in range(2):
                    rows.append(strain_ref[e, c, LAG * j : LAG * (j + 1), :])
            block = jnp.concatenate(rows, axis=0)
            at = c * 2 * NT + half * NT
            out_ref[:, at : at + NT] = block.T
        at = G_AT + c * NT
        out_ref[:, at : at + NT] = green_ref[0, c].T
    wave = resid_ref[0].astype(BF16)
    row = lax.broadcasted_iota(jnp.int32, (voxels, MAXP), 0)
    slot = lax.broadcasted_iota(jnp.int32, (voxels, MAXP), 1)
    paired = jnp.broadcast_to(events_ref[...], (voxels, MAXP))
    for m in range(EVENTS // 8):
        match = (paired == 8 * m + row % 8) & (slot < counts_ref[0])
        picked = jnp.dot(match.astype(F32).astype(BF16), wave, preferred_element_type=F32)
        out_ref[:, R_AT + m * NT : R_AT + (m + 1) * NT] = picked.astype(BF16)


def pack(green, strain, events, counts, resid):
    voxels = green.shape[-1]
    vmem = pl.BlockSpec(memory_space=pltpu.VMEM)
    return pl.pallas_call(
        pack_kernel,
        out_shape=jax.ShapeDtypeStruct((voxels, COLS), BF16),
        in_specs=[pl.BlockSpec(memory_space=pltpu.SMEM), vmem, vmem, vmem, vmem],
        out_specs=vmem,
        compiler_params=pltpu.CompilerParams(vmem_limit_bytes=32 << 20),
        name="pack",
    )(counts, green, strain, events, resid)


def product_kernel(y_ref, out_ref, x_ref, w_ref, acc_ref):
    lane = lax.broadcasted_iota(jnp.int32, (8, 128), 1)
    low = lane < 64
    for at in range(STA // 2):
        for jj in range(BLOCKS // 2):
            for cc in range(COMP // 2):
                first, second = ([], [])
                for c in (2 * cc, 2 * cc + 1):
                    col = c * 2 * NT + jj * 128
                    a = y_ref[2 * at, :, col : col + 128].astype(F32)
                    b = y_ref[2 * at + 1, :, col : col + 128].astype(F32)
                    crossed = pltpu.roll(jnp.where(low, b, a), 64, 1)
                    first.append(jnp.where(low, a, crossed))
                    second.append(jnp.where(low, crossed, b))
                for j, pair in ((2 * jj, first), (2 * jj + 1, second)):
                    r = (j * COMP + 2 * cc) * OWN
                    x_ref[r : r + 16, at * 128 : at * 128 + 128] = jnp.concatenate(pair, axis=0).astype(BF16)

    upper = lax.broadcasted_iota(jnp.int32, (LAG, NT), 1) >= lax.broadcasted_iota(jnp.int32, (LAG, NT), 0)
    wide = lax.broadcasted_iota(jnp.int32, (COMP * OWN, NT), 1)

    def build(s, slot):
        for m in range(EVENTS // 8):
            waves = y_ref[s, :, R_AT + m * NT : R_AT + (m + 1) * NT].astype(F32)
            for q in range(8):
                wave = jnp.broadcast_to(waves[q : q + 1, :], (LAG, NT))
                shifted = pltpu.roll(wave, 0, 1, stride=1, stride_axis=0)
                at = (8 * m + q) * LAG
                w_ref[slot, at : at + LAG, :] = jnp.where(upper, shifted, 0.0).astype(BF16)

    build(0, 0)
    acc_ref[...] = jnp.zeros_like(acc_ref)

    def step(s, carry):
        slot = lax.rem(s, 2)
        build(jnp.minimum(s + 1, STA - 1), 1 - slot)
        half = COMP * OWN * BLOCKS // 2
        near = jnp.dot(x_ref[:half, :], w_ref[slot], preferred_element_type=F32)
        far = jnp.dot(x_ref[half:, :], w_ref[slot, :, :128], preferred_element_type=F32)
        green = jnp.concatenate(
            [y_ref[s, :, G_AT + c * NT : G_AT + (c + 1) * NT].astype(F32) for c in range(COMP)], axis=0
        )
        total = acc_ref[...]
        for j in range(BLOCKS // 2):
            later = green
            if j:
                later = jnp.where(wide < NT - LAG * j, pltpu.roll(green, NT - LAG * j, 1), 0.0)
            rows = slice(j * COMP * OWN, (j + 1) * COMP * OWN)
            terms = near[rows] * later
            terms = terms[:, :128] + terms[:, 128:] + far[rows] * later[:, 128:]
            for c in range(COMP):
                total = total + terms[c * OWN : (c + 1) * OWN]
        acc_ref[...] = total
        return carry

    lax.fori_loop(0, STA, step, 0)
    sums = jnp.sum(acc_ref[...], axis=1, keepdims=True)
    row = lax.broadcasted_iota(jnp.int32, (8, 128), 0)
    spread = jnp.sum(jnp.where(row == lane, sums, 0.0), axis=0, keepdims=True)
    out_ref[...] = spread[:, :OWN]


def product(arrived):
    vmem = pl.BlockSpec(memory_space=pltpu.VMEM)
    width = COMP * OWN * BLOCKS
    return pl.pallas_call(
        product_kernel,
        out_shape=jax.ShapeDtypeStruct((1, OWN), F32),
        in_specs=[vmem],
        out_specs=vmem,
        scratch_shapes=[
            pltpu.VMEM((width, EVENTS * LAG), BF16),
            pltpu.VMEM((2, EVENTS * LAG, NT), BF16),
            pltpu.VMEM((OWN, 128), F32),
        ],
        compiler_params=pltpu.CompilerParams(vmem_limit_bytes=32 << 20),
        name="product",
    )(arrived)


def body(green_tensor, strain, pair_events, pair_counts, residuals):
    packed = pack(green_tensor, strain, pair_events, pair_counts, residuals)
    tiles = packed.reshape(STA, OWN, COLS)
    arrived = lax.all_to_all(tiles, "sta", split_axis=0, concat_axis=0, tiled=True)
    return product(arrived).reshape(OWN)


def solution(mesh):
    in_specs = (
        P("sta", None, None, "vox"),
        P("sta", None, None, "vox"),
        P("sta", None),
        P("sta"),
        P("sta", None, None),
    )
    out_specs = P(("vox", "sta"))
    return jax.shard_map(body, mesh=mesh, in_specs=in_specs, out_specs=out_specs, check_vma=False)
```

```python
import jax
import jax.numpy as jnp
from jax import lax
from jax.experimental import pallas as pl
from jax.experimental.pallas import tpu as pltpu
from jax.sharding import PartitionSpec as P

COMP = 6
NT = 256
STA = 16
MAXP = 32
EVENTS = 32
OWN = 8
LAG = 32
BLOCKS = NT // LAG
S_COLS = COMP * 2 * NT
G_AT = S_COLS
R_AT = G_AT + COMP * NT
COLS = R_AT + (EVENTS // 8) * NT
F32 = jnp.float32
BF16 = jnp.bfloat16


def pack_kernel(
    counts_hbm, green_hbm, strain_hbm, events_hbm, resid_hbm, out_ref,
    count_ref, green_ref, strain_ref, events_ref, resid_ref, small_sem, green_sem, strain_sem,
):
    small = [
        pltpu.make_async_copy(counts_hbm, count_ref, small_sem.at[0]),
        pltpu.make_async_copy(events_hbm, events_ref, small_sem.at[1]),
        pltpu.make_async_copy(resid_hbm, resid_ref, small_sem.at[2]),
    ]
    greens = [
        pltpu.make_async_copy(green_hbm.at[:, c], green_ref.at[:, c], green_sem.at[c]) for c in range(COMP)
    ]
    strains = [
        pltpu.make_async_copy(strain_hbm.at[:, c], strain_ref.at[:, c], strain_sem.at[c]) for c in range(COMP)
    ]
    for copy in small:
        copy.start()
    for c in range(COMP):
        strains[c].start()
        greens[c].start()
    for copy in small:
        copy.wait()
    voxels = green_ref.shape[-1]
    wave = resid_ref[0].astype(BF16)
    row = lax.broadcasted_iota(jnp.int32, (voxels, MAXP), 0)
    slot = lax.broadcasted_iota(jnp.int32, (voxels, MAXP), 1)
    paired = jnp.broadcast_to(events_ref[...], (voxels, MAXP))
    for m in range(EVENTS // 8):
        match = (paired == 8 * m + row % 8) & (slot < count_ref[0])
        picked = jnp.dot(match.astype(F32).astype(BF16), wave, preferred_element_type=F32)
        out_ref[:, R_AT + m * NT : R_AT + (m + 1) * NT] = picked.astype(BF16)
    for c in range(COMP):
        strains[c].wait()
        for half in range(2):
            rows = []
            for j in range(half * BLOCKS // 2, (half + 1) * BLOCKS // 2):
                for e in range(2):
                    rows.append(strain_ref[e, c, LAG * j : LAG * (j + 1), :])
            block = jnp.concatenate(rows, axis=0)
            at = c * 2 * NT + half * NT
            out_ref[:, at : at + NT] = block.T
        greens[c].wait()
        at = G_AT + c * NT
        out_ref[:, at : at + NT] = green_ref[0, c].T


def pack(green, strain, events, counts, resid):
    voxels = green.shape[-1]
    whole = pl.BlockSpec(memory_space=pltpu.HBM)
    return pl.pallas_call(
        pack_kernel,
        out_shape=jax.ShapeDtypeStruct((voxels, COLS), BF16),
        in_specs=[whole] * 5,
        out_specs=pl.BlockSpec(memory_space=pltpu.VMEM),
        scratch_shapes=[
            pltpu.SMEM(counts.shape, counts.dtype),
            pltpu.VMEM(green.shape, green.dtype),
            pltpu.VMEM(strain.shape, strain.dtype),
            pltpu.VMEM(events.shape, events.dtype),
            pltpu.VMEM(resid.shape, resid.dtype),
            pltpu.SemaphoreType.DMA((3,)),
            pltpu.SemaphoreType.DMA((COMP,)),
            pltpu.SemaphoreType.DMA((COMP,)),
        ],
        compiler_params=pltpu.CompilerParams(vmem_limit_bytes=48 << 20),
        name="pack",
    )(counts, *[pltpu.with_memory_space_constraint(a, pltpu.HBM) for a in (green, strain, events, resid)])


def product_kernel(y_ref, out_ref, x_ref, *w_refs):
    lane = lax.broadcasted_iota(jnp.int32, (8, 128), 1)
    low = lane < 64
    for at in range(STA // 2):
        for jj in range(BLOCKS // 2):
            for cc in range(COMP // 2):
                first, second = ([], [])
                for c in (2 * cc, 2 * cc + 1):
                    col = c * 2 * NT + jj * 128
                    a = y_ref[2 * at, :, col : col + 128].astype(F32)
                    b = y_ref[2 * at + 1, :, col : col + 128].astype(F32)
                    crossed = pltpu.roll(jnp.where(low, b, a), 64, 1)
                    first.append(jnp.where(low, a, crossed))
                    second.append(jnp.where(low, crossed, b))
                for j, pair in ((2 * jj, first), (2 * jj + 1, second)):
                    r = (j * COMP + 2 * cc) * OWN
                    x_ref[r : r + 16, at * 128 : at * 128 + 128] = jnp.concatenate(pair, axis=0).astype(BF16)

    upper = lax.broadcasted_iota(jnp.int32, (LAG, NT), 1) >= lax.broadcasted_iota(jnp.int32, (LAG, NT), 0)
    wide = lax.broadcasted_iota(jnp.int32, (COMP * OWN, NT), 1)

    def build(s, w_ref):
        for m in range(EVENTS // 8):
            waves = y_ref[s, :, R_AT + m * NT : R_AT + (m + 1) * NT].astype(F32)
            for q in range(8):
                wave = jnp.broadcast_to(waves[q : q + 1, :], (LAG, NT))
                shifted = pltpu.roll(wave, 0, 1, stride=1, stride_axis=0)
                at = (8 * m + q) * LAG
                w_ref[at : at + LAG, :] = jnp.where(upper, shifted, 0.0).astype(BF16)

    def station(s, w_ref, total):
        half = COMP * OWN * BLOCKS // 2
        both = jnp.dot(x_ref[...], w_ref[...], preferred_element_type=F32)
        green = jnp.concatenate(
            [y_ref[s, :, G_AT + c * NT : G_AT + (c + 1) * NT].astype(F32) for c in range(COMP)], axis=0
        )
        for j in range(BLOCKS // 2):
            later = green
            if j:
                later = jnp.where(wide < NT - LAG * j, pltpu.roll(green, NT - LAG * j, 1), 0.0)
            near = both[j * COMP * OWN : (j + 1) * COMP * OWN]
            far = both[half + j * COMP * OWN : half + (j + 1) * COMP * OWN, :128]
            terms = near * later
            terms = terms[:, :128] + terms[:, 128:] + far * later[:, 128:]
            for c in range(COMP):
                total = total + terms[c * OWN : (c + 1) * OWN]
        return total

    total = jnp.zeros((OWN, 128), F32)
    build(0, w_refs[0])
    for s in range(STA):
        if s + 1 < STA:
            build(s + 1, w_refs[(s + 1) % 2])
        total = station(s, w_refs[s % 2], total)
    sums = jnp.sum(total, axis=1, keepdims=True)
    row = lax.broadcasted_iota(jnp.int32, (8, 128), 0)
    spread = jnp.sum(jnp.where(row == lane, sums, 0.0), axis=0, keepdims=True)
    out_ref[...] = spread[:, :OWN]


def product(arrived):
    vmem = pl.BlockSpec(memory_space=pltpu.VMEM)
    width = COMP * OWN * BLOCKS
    return pl.pallas_call(
        product_kernel,
        out_shape=jax.ShapeDtypeStruct((1, OWN), F32),
        in_specs=[vmem],
        out_specs=vmem,
        scratch_shapes=[
            pltpu.VMEM((width, EVENTS * LAG), BF16),
            pltpu.VMEM((EVENTS * LAG, NT), BF16),
            pltpu.VMEM((EVENTS * LAG, NT), BF16),
        ],
        compiler_params=pltpu.CompilerParams(vmem_limit_bytes=32 << 20),
        name="product",
    )(arrived)


def body(green_tensor, strain, pair_events, pair_counts, residuals):
    packed = pack(green_tensor, strain, pair_events, pair_counts, residuals)
    tiles = packed.reshape(STA, OWN, COLS)
    arrived = lax.all_to_all(tiles, "sta", split_axis=0, concat_axis=0, tiled=True)
    return product(arrived).reshape(OWN)


def solution(mesh):
    in_specs = (
        P("sta", None, None, "vox"),
        P("sta", None, None, "vox"),
        P("sta", None),
        P("sta"),
        P("sta", None, None),
    )
    out_specs = P(("vox", "sta"))
    return jax.shard_map(body, mesh=mesh, in_specs=in_specs, out_specs=out_specs, check_vma=False)
```

```python
import jax
import jax.numpy as jnp
from jax import lax
from jax.experimental import pallas as pl
from jax.experimental.pallas import tpu as pltpu
from jax.sharding import PartitionSpec as P

COMP = 6
NT = 256
STA = 16
MAXP = 32
EVENTS = 32
OWN = 8
LAG = 32
BLOCKS = NT // LAG
S_COLS = COMP * 2 * NT
G_AT = S_COLS
R_AT = G_AT + COMP * NT
COLS = R_AT + (EVENTS // 8) * NT
F32 = jnp.float32
BF16 = jnp.bfloat16


def pack_kernel(
    counts_hbm, green_hbm, strain_hbm, events_hbm, resid_hbm, out_ref,
    count_ref, green_ref, strain_ref, events_ref, resid_ref, small_sem, large_sem,
):
    small = [
        pltpu.make_async_copy(counts_hbm, count_ref, small_sem.at[0]),
        pltpu.make_async_copy(events_hbm, events_ref, small_sem.at[1]),
        pltpu.make_async_copy(resid_hbm, resid_ref, small_sem.at[2]),
    ]
    strain_copy = pltpu.make_async_copy(strain_hbm, strain_ref, large_sem.at[0])
    green_copy = pltpu.make_async_copy(green_hbm, green_ref, large_sem.at[1])
    for copy in small:
        copy.start()
    strain_copy.start()
    green_copy.start()
    for copy in small:
        copy.wait()
    voxels = green_ref.shape[-1]
    wave = resid_ref[0].astype(BF16)
    row = lax.broadcasted_iota(jnp.int32, (voxels, MAXP), 0)
    slot = lax.broadcasted_iota(jnp.int32, (voxels, MAXP), 1)
    paired = jnp.broadcast_to(events_ref[...], (voxels, MAXP))
    for m in range(EVENTS // 8):
        match = (paired == 8 * m + row % 8) & (slot < count_ref[0])
        picked = jnp.dot(match.astype(F32).astype(BF16), wave, preferred_element_type=F32)
        out_ref[:, R_AT + m * NT : R_AT + (m + 1) * NT] = picked.astype(BF16)
    strain_copy.wait()
    for c in range(COMP):
        for half in range(2):
            rows = []
            for j in range(half * BLOCKS // 2, (half + 1) * BLOCKS // 2):
                for e in range(2):
                    rows.append(strain_ref[e, c, LAG * j : LAG * (j + 1), :])
            block = jnp.concatenate(rows, axis=0)
            at = c * 2 * NT + half * NT
            out_ref[:, at : at + NT] = block.T
    green_copy.wait()
    for c in range(COMP):
        at = G_AT + c * NT
        out_ref[:, at : at + NT] = green_ref[0, c].T


def pack(green, strain, events, counts, resid):
    voxels = green.shape[-1]
    whole = pl.BlockSpec(memory_space=pltpu.HBM)
    return pl.pallas_call(
        pack_kernel,
        out_shape=jax.ShapeDtypeStruct((voxels, COLS), BF16),
        in_specs=[whole] * 5,
        out_specs=pl.BlockSpec(memory_space=pltpu.VMEM),
        scratch_shapes=[
            pltpu.SMEM(counts.shape, counts.dtype),
            pltpu.VMEM(green.shape, green.dtype),
            pltpu.VMEM(strain.shape, strain.dtype),
            pltpu.VMEM(events.shape, events.dtype),
            pltpu.VMEM(resid.shape, resid.dtype),
            pltpu.SemaphoreType.DMA((3,)),
            pltpu.SemaphoreType.DMA((2,)),
        ],
        compiler_params=pltpu.CompilerParams(vmem_limit_bytes=48 << 20),
        name="pack",
    )(counts, *[pltpu.with_memory_space_constraint(a, pltpu.HBM) for a in (green, strain, events, resid)])


def product_kernel(y_ref, out_ref, x_ref, *w_refs):
    lane = lax.broadcasted_iota(jnp.int32, (8, 128), 1)
    low = lane < 64
    for at in range(STA // 2):
        for jj in range(BLOCKS // 2):
            for cc in range(COMP // 2):
                first, second = ([], [])
                for c in (2 * cc, 2 * cc + 1):
                    col = c * 2 * NT + jj * 128
                    a = y_ref[2 * at, :, col : col + 128].astype(F32)
                    b = y_ref[2 * at + 1, :, col : col + 128].astype(F32)
                    crossed = pltpu.roll(jnp.where(low, b, a), 64, 1)
                    first.append(jnp.where(low, a, crossed))
                    second.append(jnp.where(low, crossed, b))
                for j, pair in ((2 * jj, first), (2 * jj + 1, second)):
                    r = (j * COMP + 2 * cc) * OWN
                    x_ref[r : r + 16, at * 128 : at * 128 + 128] = jnp.concatenate(pair, axis=0).astype(BF16)

    upper = lax.broadcasted_iota(jnp.int32, (LAG, NT), 1) >= lax.broadcasted_iota(jnp.int32, (LAG, NT), 0)
    wide = lax.broadcasted_iota(jnp.int32, (COMP * OWN, NT), 1)

    def build(s, w_ref):
        for m in range(EVENTS // 8):
            waves = y_ref[s, :, R_AT + m * NT : R_AT + (m + 1) * NT].astype(F32)
            for q in range(8):
                wave = jnp.broadcast_to(waves[q : q + 1, :], (LAG, NT))
                shifted = pltpu.roll(wave, 0, 1, stride=1, stride_axis=0)
                at = (8 * m + q) * LAG
                w_ref[at : at + LAG, :] = jnp.where(upper, shifted, 0.0).astype(BF16)

    def station(s, w_ref, total):
        half = COMP * OWN * BLOCKS // 2
        both = jnp.dot(x_ref[...], w_ref[...], preferred_element_type=F32)
        green = jnp.concatenate(
            [y_ref[s, :, G_AT + c * NT : G_AT + (c + 1) * NT].astype(F32) for c in range(COMP)], axis=0
        )
        for j in range(BLOCKS // 2):
            later = green
            if j:
                later = jnp.where(wide < NT - LAG * j, pltpu.roll(green, NT - LAG * j, 1), 0.0)
            near = both[j * COMP * OWN : (j + 1) * COMP * OWN]
            far = both[half + j * COMP * OWN : half + (j + 1) * COMP * OWN, :128]
            terms = near * later
            terms = terms[:, :128] + terms[:, 128:] + far * later[:, 128:]
            for c in range(COMP):
                total = total + terms[c * OWN : (c + 1) * OWN]
        return total

    total = jnp.zeros((OWN, 128), F32)
    build(0, w_refs[0])
    for s in range(STA):
        if s + 1 < STA:
            build(s + 1, w_refs[(s + 1) % 2])
        total = station(s, w_refs[s % 2], total)
    sums = jnp.sum(total, axis=1, keepdims=True)
    row = lax.broadcasted_iota(jnp.int32, (8, 128), 0)
    spread = jnp.sum(jnp.where(row == lane, sums, 0.0), axis=0, keepdims=True)
    out_ref[...] = spread[:, :OWN]


def product(arrived):
    vmem = pl.BlockSpec(memory_space=pltpu.VMEM)
    width = COMP * OWN * BLOCKS
    return pl.pallas_call(
        product_kernel,
        out_shape=jax.ShapeDtypeStruct((1, OWN), F32),
        in_specs=[vmem],
        out_specs=vmem,
        scratch_shapes=[
            pltpu.VMEM((width, EVENTS * LAG), BF16),
            pltpu.VMEM((EVENTS * LAG, NT), BF16),
            pltpu.VMEM((EVENTS * LAG, NT), BF16),
        ],
        compiler_params=pltpu.CompilerParams(vmem_limit_bytes=32 << 20),
        name="product",
    )(arrived)


def body(green_tensor, strain, pair_events, pair_counts, residuals):
    packed = pack(green_tensor, strain, pair_events, pair_counts, residuals)
    tiles = packed.reshape(STA, OWN, COLS)
    arrived = lax.all_to_all(tiles, "sta", split_axis=0, concat_axis=0, tiled=True)
    return product(arrived).reshape(OWN)


def solution(mesh):
    in_specs = (
        P("sta", None, None, "vox"),
        P("sta", None, None, "vox"),
        P("sta", None),
        P("sta"),
        P("sta", None, None),
    )
    out_specs = P(("vox", "sta"))
    return jax.shard_map(body, mesh=mesh, in_specs=in_specs, out_specs=out_specs, check_vma=False)
```

```python
import jax
import jax.numpy as jnp
from jax import lax
from jax.experimental import pallas as pl
from jax.experimental.pallas import tpu as pltpu
from jax.sharding import PartitionSpec as P

COMP = 6
NT = 256
STA = 16
MAXP = 32
EVENTS = 32
OWN = 8
LAG = 32
BLOCKS = NT // LAG
S_COLS = COMP * 2 * NT
G_AT = S_COLS
R_AT = G_AT + COMP * NT
COLS = R_AT + (EVENTS // 8) * NT
ORDER = (12, 4, 5, 0, 9, 3, 1, 10, 7, 14, 2, 11, 6, 15, 13, 8)
F32 = jnp.float32
BF16 = jnp.bfloat16


def pack_kernel(
    counts_hbm, green_hbm, strain_hbm, events_hbm, resid_hbm, out_ref,
    count_ref, green_ref, strain_ref, events_ref, resid_ref, small_sem, large_sem,
):
    small = [
        pltpu.make_async_copy(counts_hbm, count_ref, small_sem.at[0]),
        pltpu.make_async_copy(events_hbm, events_ref, small_sem.at[1]),
        pltpu.make_async_copy(resid_hbm, resid_ref, small_sem.at[2]),
    ]
    strain_copy = pltpu.make_async_copy(strain_hbm, strain_ref, large_sem.at[0])
    green_copy = pltpu.make_async_copy(green_hbm, green_ref, large_sem.at[1])
    for copy in small:
        copy.start()
    strain_copy.start()
    green_copy.start()
    for copy in small:
        copy.wait()
    voxels = green_ref.shape[-1]

    def put(at, rows):
        for i, member in enumerate(ORDER):
            out_ref[i, :, at : at + NT] = rows[member * OWN : (member + 1) * OWN].astype(BF16)

    wave = resid_ref[0].astype(BF16)
    row = lax.broadcasted_iota(jnp.int32, (voxels, MAXP), 0)
    slot = lax.broadcasted_iota(jnp.int32, (voxels, MAXP), 1)
    paired = jnp.broadcast_to(events_ref[...], (voxels, MAXP))
    for m in range(EVENTS // 8):
        match = (paired == 8 * m + row % 8) & (slot < count_ref[0])
        picked = jnp.dot(match.astype(F32).astype(BF16), wave, preferred_element_type=F32)
        put(R_AT + m * NT, picked)
    strain_copy.wait()
    for c in range(COMP):
        for half in range(2):
            rows = []
            for j in range(half * BLOCKS // 2, (half + 1) * BLOCKS // 2):
                for e in range(2):
                    rows.append(strain_ref[e, c, LAG * j : LAG * (j + 1), :])
            block = jnp.concatenate(rows, axis=0)
            at = c * 2 * NT + half * NT
            put(at, block.T)
    green_copy.wait()
    for c in range(COMP):
        at = G_AT + c * NT
        put(at, green_ref[0, c].T)


def pack(green, strain, events, counts, resid):
    whole = pl.BlockSpec(memory_space=pltpu.HBM)
    return pl.pallas_call(
        pack_kernel,
        out_shape=jax.ShapeDtypeStruct((STA, OWN, COLS), BF16),
        in_specs=[whole] * 5,
        out_specs=pl.BlockSpec(memory_space=pltpu.VMEM),
        scratch_shapes=[
            pltpu.SMEM(counts.shape, counts.dtype),
            pltpu.VMEM(green.shape, green.dtype),
            pltpu.VMEM(strain.shape, strain.dtype),
            pltpu.VMEM(events.shape, events.dtype),
            pltpu.VMEM(resid.shape, resid.dtype),
            pltpu.SemaphoreType.DMA((3,)),
            pltpu.SemaphoreType.DMA((2,)),
        ],
        compiler_params=pltpu.CompilerParams(vmem_limit_bytes=48 << 20),
        name="pack",
    )(counts, *[pltpu.with_memory_space_constraint(a, pltpu.HBM) for a in (green, strain, events, resid)])


def product_kernel(y_ref, out_ref, x_ref, *w_refs):
    lane = lax.broadcasted_iota(jnp.int32, (8, 128), 1)
    low = lane < 64
    for at in range(STA // 2):
        for jj in range(BLOCKS // 2):
            for cc in range(COMP // 2):
                first, second = ([], [])
                for c in (2 * cc, 2 * cc + 1):
                    col = c * 2 * NT + jj * 128
                    a = y_ref[2 * at, :, col : col + 128].astype(F32)
                    b = y_ref[2 * at + 1, :, col : col + 128].astype(F32)
                    crossed = pltpu.roll(jnp.where(low, b, a), 64, 1)
                    first.append(jnp.where(low, a, crossed))
                    second.append(jnp.where(low, crossed, b))
                for j, pair in ((2 * jj, first), (2 * jj + 1, second)):
                    r = (j * COMP + 2 * cc) * OWN
                    x_ref[r : r + 16, at * 128 : at * 128 + 128] = jnp.concatenate(pair, axis=0).astype(BF16)

    upper = lax.broadcasted_iota(jnp.int32, (LAG, NT), 1) >= lax.broadcasted_iota(jnp.int32, (LAG, NT), 0)
    wide = lax.broadcasted_iota(jnp.int32, (COMP * OWN, NT), 1)

    def build(s, w_ref):
        for m in range(EVENTS // 8):
            waves = y_ref[s, :, R_AT + m * NT : R_AT + (m + 1) * NT].astype(F32)
            for q in range(8):
                wave = jnp.broadcast_to(waves[q : q + 1, :], (LAG, NT))
                shifted = pltpu.roll(wave, 0, 1, stride=1, stride_axis=0)
                e = 8 * m + q
                at = (2 * ORDER.index(e // 2) + e % 2) * LAG
                w_ref[at : at + LAG, :] = jnp.where(upper, shifted, 0.0).astype(BF16)

    def station(s, w_ref, total):
        half = COMP * OWN * BLOCKS // 2
        both = jnp.dot(x_ref[...], w_ref[...], preferred_element_type=F32)
        green = jnp.concatenate(
            [y_ref[s, :, G_AT + c * NT : G_AT + (c + 1) * NT].astype(F32) for c in range(COMP)], axis=0
        )
        for j in range(BLOCKS // 2):
            later = green
            if j:
                later = jnp.where(wide < NT - LAG * j, pltpu.roll(green, NT - LAG * j, 1), 0.0)
            near = both[j * COMP * OWN : (j + 1) * COMP * OWN]
            far = both[half + j * COMP * OWN : half + (j + 1) * COMP * OWN, :128]
            terms = near * later
            terms = terms[:, :128] + terms[:, 128:] + far * later[:, 128:]
            for c in range(COMP):
                total = total + terms[c * OWN : (c + 1) * OWN]
        return total

    total = jnp.zeros((OWN, 128), F32)
    build(0, w_refs[0])
    for s in range(STA):
        if s + 1 < STA:
            build(s + 1, w_refs[(s + 1) % 2])
        total = station(s, w_refs[s % 2], total)
    sums = jnp.sum(total, axis=1, keepdims=True)
    row = lax.broadcasted_iota(jnp.int32, (8, 128), 0)
    spread = jnp.sum(jnp.where(row == lane, sums, 0.0), axis=0, keepdims=True)
    out_ref[...] = spread[:, :OWN]


def product(arrived):
    vmem = pl.BlockSpec(memory_space=pltpu.VMEM)
    width = COMP * OWN * BLOCKS
    return pl.pallas_call(
        product_kernel,
        out_shape=jax.ShapeDtypeStruct((1, OWN), F32),
        in_specs=[vmem],
        out_specs=vmem,
        scratch_shapes=[
            pltpu.VMEM((width, EVENTS * LAG), BF16),
            pltpu.VMEM((EVENTS * LAG, NT), BF16),
            pltpu.VMEM((EVENTS * LAG, NT), BF16),
        ],
        compiler_params=pltpu.CompilerParams(vmem_limit_bytes=32 << 20),
        name="product",
    )(arrived)


def body(green_tensor, strain, pair_events, pair_counts, residuals):
    packed = pack(green_tensor, strain, pair_events, pair_counts, residuals)
    arrived = lax.all_to_all(
        packed, "sta", split_axis=0, concat_axis=0, tiled=True, axis_index_groups=[list(ORDER)]
    )
    return product(arrived).reshape(OWN)


def solution(mesh):
    in_specs = (
        P("sta", None, None, "vox"),
        P("sta", None, None, "vox"),
        P("sta", None),
        P("sta"),
        P("sta", None, None),
    )
    out_specs = P(("vox", "sta"))
    return jax.shard_map(body, mesh=mesh, in_specs=in_specs, out_specs=out_specs, check_vma=False)
```

```python
import jax
import jax.numpy as jnp
from jax import lax
from jax.experimental import pallas as pl
from jax.experimental.pallas import tpu as pltpu
from jax.sharding import PartitionSpec as P

COMP = 6
NT = 256
STA = 16
MAXP = 32
EVENTS = 32
OWN = 8
LAG = 32
BLOCKS = NT // LAG
S_COLS = COMP * 2 * NT
G_AT = S_COLS
R_AT = G_AT + COMP * NT
COLS = R_AT + (EVENTS // 8) * NT
ORDER = (12, 14, 6, 7, 2, 8, 5, 13, 1, 0, 11, 15, 4, 3, 9, 10)
F32 = jnp.float32
BF16 = jnp.bfloat16


def pack_kernel(
    counts_hbm, green_hbm, strain_hbm, events_hbm, resid_hbm, out_ref,
    count_ref, green_ref, strain_ref, events_ref, resid_ref, small_sem, large_sem,
):
    small = [
        pltpu.make_async_copy(counts_hbm, count_ref, small_sem.at[0]),
        pltpu.make_async_copy(events_hbm, events_ref, small_sem.at[1]),
        pltpu.make_async_copy(resid_hbm, resid_ref, small_sem.at[2]),
    ]
    strain_copy = pltpu.make_async_copy(strain_hbm, strain_ref, large_sem.at[0])
    green_copy = pltpu.make_async_copy(green_hbm, green_ref, large_sem.at[1])
    for copy in small:
        copy.start()
    green_copy.start()
    strain_copy.start()
    for copy in small:
        copy.wait()
    voxels = green_ref.shape[-1]

    def put(at, rows):
        for i, member in enumerate(ORDER):
            out_ref[i, :, at : at + NT] = rows[member * OWN : (member + 1) * OWN].astype(BF16)

    wave = resid_ref[0].astype(BF16)
    row = lax.broadcasted_iota(jnp.int32, (voxels, MAXP), 0)
    slot = lax.broadcasted_iota(jnp.int32, (voxels, MAXP), 1)
    paired = jnp.broadcast_to(events_ref[...], (voxels, MAXP))
    for m in range(EVENTS // 8):
        match = (paired == 8 * m + row % 8) & (slot < count_ref[0])
        picked = jnp.dot(match.astype(F32).astype(BF16), wave, preferred_element_type=F32)
        put(R_AT + m * NT, picked)
    green_copy.wait()
    for c in range(COMP):
        at = G_AT + c * NT
        put(at, green_ref[0, c].T)
    strain_copy.wait()
    for c in range(COMP):
        for half in range(2):
            rows = []
            for j in range(half * BLOCKS // 2, (half + 1) * BLOCKS // 2):
                for e in range(2):
                    rows.append(strain_ref[e, c, LAG * j : LAG * (j + 1), :])
            block = jnp.concatenate(rows, axis=0)
            at = c * 2 * NT + half * NT
            put(at, block.T)


def pack(green, strain, events, counts, resid):
    whole = pl.BlockSpec(memory_space=pltpu.HBM)
    return pl.pallas_call(
        pack_kernel,
        out_shape=jax.ShapeDtypeStruct((STA, OWN, COLS), BF16),
        in_specs=[whole] * 5,
        out_specs=pl.BlockSpec(memory_space=pltpu.VMEM),
        scratch_shapes=[
            pltpu.SMEM(counts.shape, counts.dtype),
            pltpu.VMEM(green.shape, green.dtype),
            pltpu.VMEM(strain.shape, strain.dtype),
            pltpu.VMEM(events.shape, events.dtype),
            pltpu.VMEM(resid.shape, resid.dtype),
            pltpu.SemaphoreType.DMA((3,)),
            pltpu.SemaphoreType.DMA((2,)),
        ],
        compiler_params=pltpu.CompilerParams(vmem_limit_bytes=48 << 20),
        name="pack",
    )(counts, *[pltpu.with_memory_space_constraint(a, pltpu.HBM) for a in (green, strain, events, resid)])


def product_kernel(y_ref, out_ref, x_ref, *w_refs):
    lane = lax.broadcasted_iota(jnp.int32, (8, 128), 1)
    low = lane < 64
    for at in range(STA // 2):
        for jj in range(BLOCKS // 2):
            for cc in range(COMP // 2):
                first, second = ([], [])
                for c in (2 * cc, 2 * cc + 1):
                    col = c * 2 * NT + jj * 128
                    a = y_ref[2 * at, :, col : col + 128].astype(F32)
                    b = y_ref[2 * at + 1, :, col : col + 128].astype(F32)
                    crossed = pltpu.roll(jnp.where(low, b, a), 64, 1)
                    first.append(jnp.where(low, a, crossed))
                    second.append(jnp.where(low, crossed, b))
                for j, pair in ((2 * jj, first), (2 * jj + 1, second)):
                    r = (j * COMP + 2 * cc) * OWN
                    x_ref[r : r + 16, at * 128 : at * 128 + 128] = jnp.concatenate(pair, axis=0).astype(BF16)

    upper = lax.broadcasted_iota(jnp.int32, (LAG, NT), 1) >= lax.broadcasted_iota(jnp.int32, (LAG, NT), 0)
    wide = lax.broadcasted_iota(jnp.int32, (COMP * OWN, NT), 1)

    def build(s, w_ref):
        for m in range(EVENTS // 8):
            waves = y_ref[s, :, R_AT + m * NT : R_AT + (m + 1) * NT].astype(F32)
            for q in range(8):
                wave = jnp.broadcast_to(waves[q : q + 1, :], (LAG, NT))
                shifted = pltpu.roll(wave, 0, 1, stride=1, stride_axis=0)
                e = 8 * m + q
                at = (2 * ORDER.index(e // 2) + e % 2) * LAG
                w_ref[at : at + LAG, :] = jnp.where(upper, shifted, 0.0).astype(BF16)

    def station(s, w_ref, total):
        half = COMP * OWN * BLOCKS // 2
        both = jnp.dot(x_ref[...], w_ref[...], preferred_element_type=F32)
        green = jnp.concatenate(
            [y_ref[s, :, G_AT + c * NT : G_AT + (c + 1) * NT].astype(F32) for c in range(COMP)], axis=0
        )
        for j in range(BLOCKS // 2):
            later = green
            if j:
                later = jnp.where(wide < NT - LAG * j, pltpu.roll(green, NT - LAG * j, 1), 0.0)
            near = both[j * COMP * OWN : (j + 1) * COMP * OWN]
            far = both[half + j * COMP * OWN : half + (j + 1) * COMP * OWN, :128]
            terms = near * later
            terms = terms[:, :128] + terms[:, 128:] + far * later[:, 128:]
            for c in range(COMP):
                total = total + terms[c * OWN : (c + 1) * OWN]
        return total

    total = jnp.zeros((OWN, 128), F32)
    build(0, w_refs[0])
    for s in range(STA):
        if s + 1 < STA:
            build(s + 1, w_refs[(s + 1) % 2])
        total = station(s, w_refs[s % 2], total)
    sums = jnp.sum(total, axis=1, keepdims=True)
    row = lax.broadcasted_iota(jnp.int32, (8, 128), 0)
    spread = jnp.sum(jnp.where(row == lane, sums, 0.0), axis=0, keepdims=True)
    out_ref[...] = spread[:, :OWN]


def product(arrived):
    vmem = pl.BlockSpec(memory_space=pltpu.VMEM)
    width = COMP * OWN * BLOCKS
    return pl.pallas_call(
        product_kernel,
        out_shape=jax.ShapeDtypeStruct((1, OWN), F32),
        in_specs=[vmem],
        out_specs=vmem,
        scratch_shapes=[
            pltpu.VMEM((width, EVENTS * LAG), BF16),
            pltpu.VMEM((EVENTS * LAG, NT), BF16),
            pltpu.VMEM((EVENTS * LAG, NT), BF16),
        ],
        compiler_params=pltpu.CompilerParams(vmem_limit_bytes=32 << 20),
        name="product",
    )(arrived)


def body(green_tensor, strain, pair_events, pair_counts, residuals):
    packed = pack(green_tensor, strain, pair_events, pair_counts, residuals)
    arrived = lax.all_to_all(
        packed, "sta", split_axis=0, concat_axis=0, tiled=True, axis_index_groups=[list(ORDER)]
    )
    return product(arrived).reshape(OWN)


def solution(mesh):
    in_specs = (
        P("sta", None, None, "vox"),
        P("sta", None, None, "vox"),
        P("sta", None),
        P("sta"),
        P("sta", None, None),
    )
    out_specs = P(("vox", "sta"))
    return jax.shard_map(body, mesh=mesh, in_specs=in_specs, out_specs=out_specs, check_vma=False)
```

```python
import jax
import jax.numpy as jnp
from jax import lax
from jax.experimental import pallas as pl
from jax.experimental.pallas import tpu as pltpu
from jax.sharding import PartitionSpec as P

COMP = 6
NT = 256
STA = 16
MAXP = 32
EVENTS = 32
OWN = 8
LAG = 32
BLOCKS = NT // LAG
S_COLS = COMP * 2 * NT
G_AT = S_COLS
R_AT = G_AT + COMP * NT
COLS = R_AT + (EVENTS // 8) * NT
ORDER = (13, 6, 12, 8, 10, 0, 14, 9, 7, 15, 2, 4, 3, 5, 11, 1)
F32 = jnp.float32
BF16 = jnp.bfloat16


def pack_kernel(
    counts_hbm, green_hbm, strain_hbm, events_hbm, resid_hbm, out_ref,
    count_ref, green_ref, strain_ref, events_ref, resid_ref, small_sem, large_sem,
):
    small = [
        pltpu.make_async_copy(counts_hbm, count_ref, small_sem.at[0]),
        pltpu.make_async_copy(events_hbm, events_ref, small_sem.at[1]),
        pltpu.make_async_copy(resid_hbm, resid_ref, small_sem.at[2]),
    ]
    strain_copy = pltpu.make_async_copy(strain_hbm, strain_ref, large_sem.at[0])
    green_copy = pltpu.make_async_copy(green_hbm, green_ref, large_sem.at[1])
    for copy in small:
        copy.start()
    green_copy.start()
    strain_copy.start()
    for copy in small:
        copy.wait()
    voxels = green_ref.shape[-1]

    def put(at, rows):
        for i, member in enumerate(ORDER):
            out_ref[i, :, at : at + NT] = rows[member * OWN : (member + 1) * OWN].astype(BF16)

    wave = resid_ref[0].astype(BF16)
    row = lax.broadcasted_iota(jnp.int32, (voxels, MAXP), 0)
    slot = lax.broadcasted_iota(jnp.int32, (voxels, MAXP), 1)
    paired = jnp.broadcast_to(events_ref[...], (voxels, MAXP))
    for m in range(EVENTS // 8):
        match = (paired == 8 * m + row % 8) & (slot < count_ref[0])
        picked = jnp.dot(match.astype(F32).astype(BF16), wave, preferred_element_type=F32)
        put(R_AT + m * NT, picked)
    green_copy.wait()
    for c in range(COMP):
        at = G_AT + c * NT
        put(at, green_ref[0, c].T)
    strain_copy.wait()
    for c in range(COMP):
        for half in range(2):
            rows = []
            for j in range(half * BLOCKS // 2, (half + 1) * BLOCKS // 2):
                for e in range(2):
                    rows.append(strain_ref[e, c, LAG * j : LAG * (j + 1), :])
            block = jnp.concatenate(rows, axis=0)
            at = c * 2 * NT + half * NT
            put(at, block.T)


def pack(green, strain, events, counts, resid):
    whole = pl.BlockSpec(memory_space=pltpu.HBM)
    return pl.pallas_call(
        pack_kernel,
        out_shape=jax.ShapeDtypeStruct((STA, OWN, COLS), BF16),
        in_specs=[whole] * 5,
        out_specs=pl.BlockSpec(memory_space=pltpu.VMEM),
        scratch_shapes=[
            pltpu.SMEM(counts.shape, counts.dtype),
            pltpu.VMEM(green.shape, green.dtype),
            pltpu.VMEM(strain.shape, strain.dtype),
            pltpu.VMEM(events.shape, events.dtype),
            pltpu.VMEM(resid.shape, resid.dtype),
            pltpu.SemaphoreType.DMA((3,)),
            pltpu.SemaphoreType.DMA((2,)),
        ],
        compiler_params=pltpu.CompilerParams(vmem_limit_bytes=48 << 20),
        name="pack",
    )(counts, *[pltpu.with_memory_space_constraint(a, pltpu.HBM) for a in (green, strain, events, resid)])


def product_kernel(y_ref, out_ref, x_ref, *w_refs):
    lane = lax.broadcasted_iota(jnp.int32, (8, 128), 1)
    low = lane < 64
    for at in range(STA // 2):
        for jj in range(BLOCKS // 2):
            for cc in range(COMP // 2):
                first, second = ([], [])
                for c in (2 * cc, 2 * cc + 1):
                    col = c * 2 * NT + jj * 128
                    a = y_ref[2 * at, :, col : col + 128].astype(F32)
                    b = y_ref[2 * at + 1, :, col : col + 128].astype(F32)
                    crossed = pltpu.roll(jnp.where(low, b, a), 64, 1)
                    first.append(jnp.where(low, a, crossed))
                    second.append(jnp.where(low, crossed, b))
                for j, pair in ((2 * jj, first), (2 * jj + 1, second)):
                    r = (j * COMP + 2 * cc) * OWN
                    x_ref[r : r + 16, at * 128 : at * 128 + 128] = jnp.concatenate(pair, axis=0).astype(BF16)

    upper = lax.broadcasted_iota(jnp.int32, (LAG, NT), 1) >= lax.broadcasted_iota(jnp.int32, (LAG, NT), 0)
    wide = lax.broadcasted_iota(jnp.int32, (COMP * OWN, NT), 1)

    def build(s, w_ref):
        for m in range(EVENTS // 8):
            waves = y_ref[s, :, R_AT + m * NT : R_AT + (m + 1) * NT].astype(F32)
            for q in range(8):
                wave = jnp.broadcast_to(waves[q : q + 1, :], (LAG, NT))
                shifted = pltpu.roll(wave, 0, 1, stride=1, stride_axis=0)
                e = 8 * m + q
                at = (2 * ORDER.index(e // 2) + e % 2) * LAG
                w_ref[at : at + LAG, :] = jnp.where(upper, shifted, 0.0).astype(BF16)

    def station(s, w_ref, total):
        half = COMP * OWN * BLOCKS // 2
        both = jnp.dot(x_ref[...], w_ref[...], preferred_element_type=F32)
        green = jnp.concatenate(
            [y_ref[s, :, G_AT + c * NT : G_AT + (c + 1) * NT].astype(F32) for c in range(COMP)], axis=0
        )
        for j in range(BLOCKS // 2):
            later = green
            if j:
                later = jnp.where(wide < NT - LAG * j, pltpu.roll(green, NT - LAG * j, 1), 0.0)
            near = both[j * COMP * OWN : (j + 1) * COMP * OWN]
            far = both[half + j * COMP * OWN : half + (j + 1) * COMP * OWN, :128]
            terms = near * later
            terms = terms[:, :128] + terms[:, 128:] + far * later[:, 128:]
            for c in range(COMP):
                total = total + terms[c * OWN : (c + 1) * OWN]
        return total

    total = jnp.zeros((OWN, 128), F32)
    build(0, w_refs[0])
    for s in range(STA):
        if s + 1 < STA:
            build(s + 1, w_refs[(s + 1) % 2])
        total = station(s, w_refs[s % 2], total)
    sums = jnp.sum(total, axis=1, keepdims=True)
    row = lax.broadcasted_iota(jnp.int32, (8, 128), 0)
    spread = jnp.sum(jnp.where(row == lane, sums, 0.0), axis=0, keepdims=True)
    out_ref[...] = spread[:, :OWN]


def product(arrived):
    vmem = pl.BlockSpec(memory_space=pltpu.VMEM)
    width = COMP * OWN * BLOCKS
    return pl.pallas_call(
        product_kernel,
        out_shape=jax.ShapeDtypeStruct((1, OWN), F32),
        in_specs=[vmem],
        out_specs=vmem,
        scratch_shapes=[
            pltpu.VMEM((width, EVENTS * LAG), BF16),
            pltpu.VMEM((EVENTS * LAG, NT), BF16),
            pltpu.VMEM((EVENTS * LAG, NT), BF16),
        ],
        compiler_params=pltpu.CompilerParams(vmem_limit_bytes=32 << 20),
        name="product",
    )(arrived)


def body(green_tensor, strain, pair_events, pair_counts, residuals):
    packed = pack(green_tensor, strain, pair_events, pair_counts, residuals)
    arrived = lax.all_to_all(
        packed, "sta", split_axis=0, concat_axis=0, tiled=True, axis_index_groups=[list(ORDER)]
    )
    return product(arrived).reshape(OWN)


def solution(mesh):
    in_specs = (
        P("sta", None, None, "vox"),
        P("sta", None, None, "vox"),
        P("sta", None),
        P("sta"),
        P("sta", None, None),
    )
    out_specs = P(("vox", "sta"))
    return jax.shard_map(body, mesh=mesh, in_specs=in_specs, out_specs=out_specs, check_vma=False)
```

```python
import jax
import jax.numpy as jnp
from jax import lax
from jax.experimental import pallas as pl
from jax.experimental.pallas import tpu as pltpu
from jax.sharding import PartitionSpec as P

COMP = 6
NT = 256
STA = 16
MAXP = 32
EVENTS = 32
OWN = 8
LAG = 32
BLOCKS = NT // LAG
S_COLS = COMP * 2 * NT
G_AT = S_COLS
R_AT = G_AT + COMP * NT
COLS = R_AT + (EVENTS // 8) * NT
ORDER = (13, 6, 12, 8, 10, 0, 14, 9, 7, 15, 2, 4, 3, 5, 11, 1)
F32 = jnp.float32
BF16 = jnp.bfloat16


def pack_kernel(
    counts_hbm, green_hbm, strain_hbm, events_hbm, resid_hbm, out_ref,
    count_ref, green_ref, strain_ref, events_ref, resid_ref, small_sem, large_sem,
):
    small = [
        pltpu.make_async_copy(counts_hbm, count_ref, small_sem.at[0]),
        pltpu.make_async_copy(events_hbm, events_ref, small_sem.at[1]),
        pltpu.make_async_copy(resid_hbm, resid_ref, small_sem.at[2]),
    ]
    strain_copies = [
        pltpu.make_async_copy(strain_hbm.at[e], strain_ref.at[e], large_sem.at[2 * e]) for e in range(2)
    ]
    green_copy = pltpu.make_async_copy(green_hbm, green_ref, large_sem.at[1])
    for copy in small:
        copy.start()
    green_copy.start()
    for copy in strain_copies:
        copy.start()
    for copy in small:
        copy.wait()
    voxels = green_ref.shape[-1]

    def put(at, rows):
        for i, member in enumerate(ORDER):
            out_ref[i, :, at : at + NT] = rows[member * OWN : (member + 1) * OWN].astype(BF16)

    wave = resid_ref[0].astype(BF16)
    row = lax.broadcasted_iota(jnp.int32, (voxels, MAXP), 0)
    slot = lax.broadcasted_iota(jnp.int32, (voxels, MAXP), 1)
    paired = jnp.broadcast_to(events_ref[...], (voxels, MAXP))
    for m in range(EVENTS // 8):
        match = (paired == 8 * m + row % 8) & (slot < count_ref[0])
        picked = jnp.dot(match.astype(F32).astype(BF16), wave, preferred_element_type=F32)
        put(R_AT + m * NT, picked)
    green_copy.wait()
    for c in range(COMP):
        at = G_AT + c * NT
        put(at, green_ref[0, c].T)
    for copy in strain_copies:
        copy.wait()
    for c in range(COMP):
        for half in range(2):
            rows = []
            for j in range(half * BLOCKS // 2, (half + 1) * BLOCKS // 2):
                for e in range(2):
                    rows.append(strain_ref[e, c, LAG * j : LAG * (j + 1), :])
            block = jnp.concatenate(rows, axis=0)
            at = c * 2 * NT + half * NT
            put(at, block.T)


def pack(green, strain, events, counts, resid):
    whole = pl.BlockSpec(memory_space=pltpu.HBM)
    return pl.pallas_call(
        pack_kernel,
        out_shape=jax.ShapeDtypeStruct((STA, OWN, COLS), BF16),
        in_specs=[whole] * 5,
        out_specs=pl.BlockSpec(memory_space=pltpu.VMEM),
        scratch_shapes=[
            pltpu.SMEM(counts.shape, counts.dtype),
            pltpu.VMEM(green.shape, green.dtype),
            pltpu.VMEM(strain.shape, strain.dtype),
            pltpu.VMEM(events.shape, events.dtype),
            pltpu.VMEM(resid.shape, resid.dtype),
            pltpu.SemaphoreType.DMA((3,)),
            pltpu.SemaphoreType.DMA((3,)),
        ],
        compiler_params=pltpu.CompilerParams(vmem_limit_bytes=48 << 20),
        name="pack",
    )(counts, *[pltpu.with_memory_space_constraint(a, pltpu.HBM) for a in (green, strain, events, resid)])


def product_kernel(y_ref, out_ref, x_ref, *w_refs):
    lane = lax.broadcasted_iota(jnp.int32, (8, 128), 1)
    low = lane < 64
    for at in range(STA // 2):
        for jj in range(BLOCKS // 2):
            for cc in range(COMP // 2):
                first, second = ([], [])
                for c in (2 * cc, 2 * cc + 1):
                    col = c * 2 * NT + jj * 128
                    a = y_ref[2 * at, :, col : col + 128].astype(F32)
                    b = y_ref[2 * at + 1, :, col : col + 128].astype(F32)
                    crossed = pltpu.roll(jnp.where(low, b, a), 64, 1)
                    first.append(jnp.where(low, a, crossed))
                    second.append(jnp.where(low, crossed, b))
                for j, pair in ((2 * jj, first), (2 * jj + 1, second)):
                    r = (j * COMP + 2 * cc) * OWN
                    x_ref[r : r + 16, at * 128 : at * 128 + 128] = jnp.concatenate(pair, axis=0).astype(BF16)

    upper = lax.broadcasted_iota(jnp.int32, (LAG, NT), 1) >= lax.broadcasted_iota(jnp.int32, (LAG, NT), 0)
    wide = lax.broadcasted_iota(jnp.int32, (COMP * OWN, NT), 1)

    def build(s, w_ref):
        for m in range(EVENTS // 8):
            waves = y_ref[s, :, R_AT + m * NT : R_AT + (m + 1) * NT].astype(F32)
            for q in range(8):
                wave = jnp.broadcast_to(waves[q : q + 1, :], (LAG, NT))
                shifted = pltpu.roll(wave, 0, 1, stride=1, stride_axis=0)
                e = 8 * m + q
                at = (2 * ORDER.index(e // 2) + e % 2) * LAG
                w_ref[at : at + LAG, :] = jnp.where(upper, shifted, 0.0).astype(BF16)

    def station(s, w_ref, total):
        half = COMP * OWN * BLOCKS // 2
        both = jnp.dot(x_ref[...], w_ref[...], preferred_element_type=F32)
        green = jnp.concatenate(
            [y_ref[s, :, G_AT + c * NT : G_AT + (c + 1) * NT].astype(F32) for c in range(COMP)], axis=0
        )
        for j in range(BLOCKS // 2):
            later = green
            if j:
                later = jnp.where(wide < NT - LAG * j, pltpu.roll(green, NT - LAG * j, 1), 0.0)
            near = both[j * COMP * OWN : (j + 1) * COMP * OWN]
            far = both[half + j * COMP * OWN : half + (j + 1) * COMP * OWN, :128]
            terms = near * later
            terms = terms[:, :128] + terms[:, 128:] + far * later[:, 128:]
            for c in range(COMP):
                total = total + terms[c * OWN : (c + 1) * OWN]
        return total

    total = jnp.zeros((OWN, 128), F32)
    build(0, w_refs[0])
    for s in range(STA):
        if s + 1 < STA:
            build(s + 1, w_refs[(s + 1) % 2])
        total = station(s, w_refs[s % 2], total)
    sums = jnp.sum(total, axis=1, keepdims=True)
    row = lax.broadcasted_iota(jnp.int32, (8, 128), 0)
    spread = jnp.sum(jnp.where(row == lane, sums, 0.0), axis=0, keepdims=True)
    out_ref[...] = spread[:, :OWN]


def product(arrived):
    vmem = pl.BlockSpec(memory_space=pltpu.VMEM)
    width = COMP * OWN * BLOCKS
    return pl.pallas_call(
        product_kernel,
        out_shape=jax.ShapeDtypeStruct((1, OWN), F32),
        in_specs=[vmem],
        out_specs=vmem,
        scratch_shapes=[
            pltpu.VMEM((width, EVENTS * LAG), BF16),
            pltpu.VMEM((EVENTS * LAG, NT), BF16),
            pltpu.VMEM((EVENTS * LAG, NT), BF16),
        ],
        compiler_params=pltpu.CompilerParams(vmem_limit_bytes=32 << 20),
        name="product",
    )(arrived)


def body(green_tensor, strain, pair_events, pair_counts, residuals):
    packed = pack(green_tensor, strain, pair_events, pair_counts, residuals)
    arrived = lax.all_to_all(
        packed, "sta", split_axis=0, concat_axis=0, tiled=True, axis_index_groups=[list(ORDER)]
    )
    return product(arrived).reshape(OWN)


def solution(mesh):
    in_specs = (
        P("sta", None, None, "vox"),
        P("sta", None, None, "vox"),
        P("sta", None),
        P("sta"),
        P("sta", None, None),
    )
    out_specs = P(("vox", "sta"))
    return jax.shard_map(body, mesh=mesh, in_specs=in_specs, out_specs=out_specs, check_vma=False)
```
